128 devices in a mesh: rows: 8 (over z, core), seq: 16 (over x, y).
Axes of the slice: x: 4, y: 4, z: 4, core: 2. Of those that a mesh axis runs over, the one named last changes fastest.
Arguments:
- queries: bfloat16 [4096, 4096], P('seq'), may hold values from -50 to 50
- keys: bfloat16 [4096, 4096], P('seq'), may hold values from -6 to 6
- values: bfloat16 [4096, 4096], P('seq'), may hold values from -6 to 6
- grad_out: bfloat16 [8, 4096, 4096], P('rows', 'seq'), may hold values from -6 to 6
- table: bfloat16 [33, 4096], replicated, may hold values from -6 to 6
- positions: int32 [8], P('rows'), may hold values from 0 to 4095
- residues: int32 [8], P('rows'), may hold values from 4 to 23
- tiles: int32 [32, 8], replicated, may hold values from 0 to 31, as said below
- counts: int32 [32], replicated, may hold values from 1 to 8, as said below
Outputs:
- grad_queries: bfloat16 [8, 4096, 4096], P('rows', 'seq')
- grad_keys: bfloat16 [8, 4096, 4096], P('rows', 'seq')
- grad_values: bfloat16 [8, 4096, 4096], P('rows', 'seq')
The draws below stay inside these ranges and needn't reach their ends.
Inputs may be any that keep to these rules, and one draw needn't show every extreme that they name: `tiles`: row i lists key blocks: entry 0 is i itself, the others differ from i and from each other. Only the first counts[i] entries of row i of tiles are used; some query block uses all 8.
All inputs are finite; a program needn't handle non-finite values.
Results may differ from the reference program's by a relative error of at most 0.0085.
Values may be sent and summed in bfloat16 or wider, within the bound.
No kernel may reach another device: no remote copies, remote signals or barrier semaphores. Data moves between devices by JAX's collectives and lax.ppermute only.
A program may use at most 128 MiB of HBM per device.

```python
import jax
import jax.numpy as jnp
from jax import lax

HEADS = 32
D_HEAD = 128
VOCAB = 33
BLOCK = 128
TILES = 8
SEQ = 4096
ROWS = 8
D = 4096


def query_key_pair(key):
    base = jax.random.fold_in(key, 11)
    first_key, second_key = jax.random.split(base, 2)
    keys = jnp.clip(jax.random.normal(second_key, (SEQ, D)), -6.0, 6.0)
    queries = jnp.clip(jax.random.normal(first_key, (SEQ, D)), -6.0, 6.0)
    return (queries, keys)


def draw_queries(key, part):
    return query_key_pair(key)[0].astype(jnp.bfloat16)


def draw_keys(key, part):
    return query_key_pair(key)[1].astype(jnp.bfloat16)


def draw_tiles(key, part):
    block_count = SEQ // BLOCK
    scores = jax.random.randint(jax.random.fold_in(key, 3), (block_count, block_count - 1), 0, 1 << 20) * block_count
    scores = scores + jnp.arange(block_count - 1, dtype=jnp.int32)[None, :]
    order = jnp.argsort(scores, axis=1)
    offsets = order[:, :TILES - 1] + 1
    own = jnp.arange(block_count, dtype=jnp.int32)[:, None]
    others = (own + offsets) % block_count
    return jnp.concatenate([own, others], axis=1).astype(jnp.int32)


def draw_counts(key, part):
    block_count = SEQ // BLOCK
    first_key, second_key = jax.random.split(jax.random.fold_in(key, 5), 2)
    raw = jax.random.randint(first_key, (block_count,), 1, TILES + 1)
    fullest = jax.random.randint(second_key, (), 0, block_count)
    return jnp.where(jnp.arange(block_count) == fullest, TILES, raw).astype(jnp.int32)


def touch_ends(drawn, rng, low, largest):
    shape = drawn.shape
    spot = [jax.random.randint(jax.random.fold_in(rng, axis), (), 0, shape[axis]) for axis in range(len(shape))]
    drawn = drawn.at[tuple(spot)].set(low)
    longest = shape.index(max(shape))
    spot[longest] = (spot[longest] + 1) % shape[longest]
    return drawn.at[tuple(spot)].set(largest)


def block_scale(own_key, extent, shards, low, largest):
    gain, own = 1.0, jax.random.fold_in(own_key, 6)
    for position, blocks in shards:
        steps = jnp.exp(jax.random.uniform(jax.random.fold_in(own, position), (blocks,), jnp.float32, low / len(shards), largest / len(shards)))
        gain = gain * jnp.repeat(steps, extent[position] // blocks).reshape([-1 if axis == position else 1 for axis in range(len(extent))])
    return gain


def bell_draw(rng, dims, scale, reach, cuts=(), held_as=jnp.bfloat16):
    array = jax.random.normal(rng, dims, jnp.float32) * scale
    if len(cuts) > 0:
        array = block_scale(rng, dims, cuts, -0.22, 0.18) * array
    return jnp.clip(array, min=-reach, max=reach).astype(held_as)


def setup_inputs(seed: int = 0) -> dict:
    arg_keys = jax.random.split(jax.random.key(seed), 10)
    return {
        "queries": draw_queries(jax.random.fold_in(arg_keys[9], 71), 0),
        "keys": draw_keys(jax.random.fold_in(arg_keys[9], 71), 0),
        "values": bell_draw(arg_keys[2], (SEQ, D), 1.0, 6.0, ((0, 16),)),
        "grad_out": bell_draw(arg_keys[3], (ROWS, SEQ, D), 1.0, 6.0, ((0, 8), (1, 16))),
        "table": bell_draw(arg_keys[4], (VOCAB, D), 1.0, 6.0),
        "positions": touch_ends(jax.random.randint(arg_keys[5], (ROWS,), 0, SEQ), jax.random.fold_in(arg_keys[5], 1), 0, SEQ - 1).astype(jnp.int32),
        "residues": touch_ends(jax.random.randint(arg_keys[6], (ROWS,), 4, 24), jax.random.fold_in(arg_keys[6], 1), 4, 23).astype(jnp.int32),
        "tiles": draw_tiles(jax.random.fold_in(arg_keys[9], 71), 0),
        "counts": draw_counts(jax.random.fold_in(arg_keys[9], 71), 0),
    }


def substitute(grad_out, table, positions, residues, first_token):
    tok_count = grad_out.shape[1]
    spots = ((jnp.arange(tok_count, dtype=jnp.int32)[None, :] + first_token) == positions[:, None]).astype(jnp.float32)
    picks = (jnp.arange(table.shape[0], dtype=jnp.int32)[None, :] == residues[:, None]).astype(jnp.bfloat16)
    added = jnp.dot(picks, table, preferred_element_type=jnp.float32)
    summed = grad_out.astype(jnp.float32) + spots[:, :, None] * added[:, None, :]
    return summed.astype(jnp.bfloat16)


def log_total(scores):
    row_max = jnp.max(scores, axis=(-2, -1), keepdims=True)
    return row_max + jnp.log(jnp.sum(jnp.exp(scores - row_max), axis=(-2, -1), keepdims=True))


def reference(queries, keys, values, grad_out, table, positions, residues, tiles, counts):
    softmax_scale = D_HEAD ** -0.5
    block_count = SEQ // BLOCK
    cotangent = substitute(grad_out, table, positions, residues, 0)
    query_blocks = queries.reshape(block_count, BLOCK, HEADS, D_HEAD).astype(jnp.float32)
    key_blocks = keys.reshape(block_count, BLOCK, HEADS, D_HEAD).astype(jnp.float32)
    value_blocks = values.reshape(block_count, BLOCK, HEADS, D_HEAD).astype(jnp.float32)
    cot_blocks = cotangent.reshape(ROWS, block_count, BLOCK, HEADS, D_HEAD)
    slot_ids = jnp.arange(TILES, dtype=jnp.int32)

    def step(totals, block_index):
        grad_keys, grad_values = totals
        key_ids = tiles[block_index]
        live_slots = (slot_ids < counts[block_index])[None, None, :, None]
        query_now = query_blocks[block_index]
        key_tiles = key_blocks[key_ids]
        value_tiles = value_blocks[key_ids]
        cot_now = lax.dynamic_index_in_dim(cot_blocks, block_index, 1, keepdims=False).astype(jnp.float32)
        scores = jnp.einsum("qhd,tkhd->hqtk", query_now, key_tiles) * softmax_scale
        scores = jnp.where(live_slots, scores, -1e30)
        probs = jnp.where(live_slots, jnp.exp(scores - log_total(scores)), 0.0)
        probs_bf = lax.optimization_barrier(probs.astype(jnp.bfloat16)).astype(jnp.float32)
        grad_probs = jnp.einsum("rqhd,tkhd->rhqtk", cot_now, value_tiles)
        delta = jnp.sum(probs[None] * grad_probs, axis=(3, 4), keepdims=True)
        grad_scores = lax.optimization_barrier((probs[None] * (grad_probs - delta)).astype(jnp.bfloat16)).astype(jnp.float32)
        grad_query = (softmax_scale * jnp.einsum("rhqtk,tkhd->rqhd", grad_scores, key_tiles)).astype(jnp.bfloat16)
        key_terms = softmax_scale * jnp.einsum("rhqtk,qhd->rtkhd", grad_scores, query_now)
        value_terms = jnp.einsum("hqtk,rqhd->rtkhd", probs_bf, cot_now)
        grad_keys = grad_keys.at[:, key_ids].add(key_terms)
        grad_values = grad_values.at[:, key_ids].add(value_terms)
        return (grad_keys, grad_values), grad_query

    zeros_full = jnp.zeros((ROWS, block_count, BLOCK, HEADS, D_HEAD), jnp.float32)
    (grad_keys, grad_values), grad_query = lax.scan(step, (zeros_full, zeros_full), jnp.arange(block_count, dtype=jnp.int32))
    grad_queries = grad_query.transpose(1, 0, 2, 3, 4).reshape(ROWS, SEQ, D)
    grad_keys = grad_keys.reshape(ROWS, SEQ, D).astype(jnp.bfloat16)
    grad_values = grad_values.reshape(ROWS, SEQ, D).astype(jnp.bfloat16)
    return (grad_queries, grad_keys, grad_values)
```

```python
import functools
import math

import jax
import jax.numpy as jnp
from jax import lax
from jax.experimental import pallas as pl
from jax.experimental.pallas import tpu as pltpu
from jax.sharding import PartitionSpec as P

D_HEAD = 128
BLOCK = 128
TILES = 8
HEADS_LOCAL = 2
SCALE = D_HEAD ** (-0.5)
EXP_SCALE = SCALE * math.log2(math.e)


def pack_inputs(share, queries, keys, values, row_devices, seq_devices):
    toks, width = queries.shape
    rows = toks // row_devices
    wide = HEADS_LOCAL * D_HEAD

    def body(share_ref, q_ref, k_ref, v_ref, out_ref):
        for which, ref in enumerate((q_ref, k_ref, v_ref)):
            for dest in range(seq_devices):
                for head in range(HEADS_LOCAL):
                    start = dest * wide + head * D_HEAD
                    out_ref[dest, head, which] = ref[:, start : start + D_HEAD]

    spec = pl.BlockSpec((rows, width), lambda g, share_ref: (share_ref[0], 0))
    out_dims = (seq_devices, HEADS_LOCAL, 3, rows, D_HEAD)
    return pl.pallas_call(
        body,
        grid_spec=pltpu.PrefetchScalarGridSpec(
            num_scalar_prefetch=1,
            grid=(1,),
            in_specs=[spec, spec, spec],
            out_specs=pl.BlockSpec(out_dims, lambda g, share_ref: (0, 0, 0, 0, 0)),
        ),
        out_shape=jax.ShapeDtypeStruct(out_dims, jnp.bfloat16),
        name="pack_inputs",
    )(share, queries, keys, values)


def pack_cotangent(spot, grad_out, table, seq_devices):
    toks, width = grad_out.shape
    wide = HEADS_LOCAL * D_HEAD

    def body(spot_ref, g_ref, table_ref, *outs):
        local = spot_ref[0]
        residue = spot_ref[1]
        for dest in range(seq_devices):
            for head in range(HEADS_LOCAL):
                start = dest * wide + head * D_HEAD
                outs[head][dest] = g_ref[:, start : start + D_HEAD]

        @pl.when(jnp.logical_and(local >= 0, local < toks))
        def _():
            base = pl.multiple_of((local // 16) * 16, 16)
            picks = lax.broadcasted_iota(jnp.int32, (table.shape[0], D_HEAD), 0) == residue
            here = lax.broadcasted_iota(jnp.int32, (16, D_HEAD), 0) == local - base
            for dest in range(seq_devices):
                for head in range(HEADS_LOCAL):
                    start = dest * wide + head * D_HEAD
                    rows = table_ref[:, start : start + D_HEAD].astype(jnp.float32)
                    added = jnp.sum(jnp.where(picks, rows, 0.0), axis=0, keepdims=True)
                    now = g_ref[pl.ds(base, 16), start : start + D_HEAD].astype(jnp.float32)
                    outs[head][dest, pl.ds(base, 16), :] = (
                        now + jnp.where(here, added, 0.0)
                    ).astype(jnp.bfloat16)

    out_dims = (seq_devices, toks, D_HEAD)
    return pl.pallas_call(
        body,
        grid_spec=pltpu.PrefetchScalarGridSpec(
            num_scalar_prefetch=1,
            grid=(1,),
            in_specs=[
                pl.BlockSpec((toks, width), lambda g, s: (0, 0)),
                pl.BlockSpec(table.shape, lambda g, s: (0, 0)),
            ],
            out_specs=[pl.BlockSpec(out_dims, lambda g, s: (0, 0, 0))] * HEADS_LOCAL,
        ),
        out_shape=[jax.ShapeDtypeStruct(out_dims, jnp.bfloat16)] * HEADS_LOCAL,
        name="pack_cotangent",
    )(spot, grad_out, table)


def dot_nt(left, right):
    return lax.dot_general(left, right, (((1,), (1,)), ((), ())), preferred_element_type=jnp.float32)


def dot_nn(left, right):
    return lax.dot_general(left, right, (((1,), (0,)), ((), ())), preferred_element_type=jnp.float32)


def attention(head, tiles, counts, sources, pieces, spans, cot, row_devices, seq_devices):
    toks = cot.shape[1]
    rows = toks // row_devices
    block_count = seq_devices * toks // BLOCK
    per_dev = toks // BLOCK
    quarters = BLOCK // rows
    n_pieces = len(pieces)

    def body(tiles_ref, counts_ref, source_ref, *refs):
        piece_refs = refs[:n_pieces]
        cot_hbm, out_ref = refs[n_pieces : n_pieces + 2]
        q_v, k_v, v_v, c_v, kt_v, gk_v, gv_v, sem = refs[n_pieces + 2 :]
        copies = [pltpu.make_async_copy(cot_hbm, c_v, sem.at[0])]
        for p, ref in enumerate(piece_refs):
            share = source_ref[p]
            for which, dst in enumerate((q_v, k_v, v_v)):
                copies.append(
                    pltpu.make_async_copy(
                        ref.at[:, head, which],
                        dst.at[
                            pl.ds(spans[p][0], spans[p][1]), share // quarters, share % quarters
                        ],
                        sem.at[1 + 3 * p + which],
                    )
                )
        for copy in copies:
            copy.start()

        def clear(b, carry):
            gk_v[b] = jnp.zeros((BLOCK, D_HEAD), jnp.float32)
            gv_v[b] = jnp.zeros((BLOCK, D_HEAD), jnp.float32)
            return carry

        lax.fori_loop(0, block_count, clear, 0)
        for copy in copies:
            copy.wait()

        def flip(b, carry):
            block = k_v[b // per_dev, b % per_dev].reshape(BLOCK, D_HEAD)
            kt_v[b] = block.T
            return carry

        lax.fori_loop(0, block_count, flip, 0)

        def run(i, count):
            q_b = q_v[i // per_dev, i % per_dev].reshape(BLOCK, D_HEAD)
            c_b = c_v[i // per_dev, pl.ds(pl.multiple_of((i % per_dev) * BLOCK, BLOCK), BLOCK), :]
            ids = [tiles_ref[i * TILES + j] for j in range(count)]
            scores = [
                dot_nt(k_v[t // per_dev, t % per_dev].reshape(BLOCK, D_HEAD), q_b) for t in ids
            ]
            grad_probs = [
                dot_nt(v_v[t // per_dev, t % per_dev].reshape(BLOCK, D_HEAD), c_b) for t in ids
            ]
            top = functools.reduce(jnp.maximum, scores)
            top = jnp.max(top, axis=0, keepdims=True)
            probs = [jnp.exp2((s - top) * EXP_SCALE) for s in scores]
            total = jnp.sum(functools.reduce(jnp.add, probs), axis=0, keepdims=True)
            inverse = 1.0 / total
            delta = functools.reduce(jnp.add, [p * g for p, g in zip(probs, grad_probs)])
            delta = jnp.sum(delta, axis=0, keepdims=True) * inverse
            probs = [p * inverse for p in probs]
            grad_scores = [
                (p * (g - delta)).astype(jnp.bfloat16) for p, g in zip(probs, grad_probs)
            ]
            probs = [p.astype(jnp.bfloat16) for p in probs]
            grad_q = dot_nn(
                jnp.concatenate([kt_v[t] for t in ids], axis=1),
                jnp.concatenate(grad_scores, axis=0),
            )
            for t, p, g in zip(ids, probs, grad_scores):
                gv_v[t] += dot_nn(p, c_b)
                gk_v[t] += dot_nn(g, q_b)
            out_ref[
                i // per_dev, 0, pl.ds(pl.multiple_of((i % per_dev) * BLOCK, BLOCK), BLOCK), :
            ] = (grad_q.T * SCALE).astype(jnp.bfloat16)

        def step(i, carry):
            for count in range(1, TILES + 1):

                @pl.when(counts_ref[i] == count)
                def _(count=count):
                    run(i, count)

            return carry

        lax.fori_loop(0, block_count, step, 0)

        def finish(b, carry):
            at = pl.ds(pl.multiple_of((b % per_dev) * BLOCK, BLOCK), BLOCK)
            out_ref[b // per_dev, 1, at, :] = (gk_v[b] * SCALE).astype(jnp.bfloat16)
            out_ref[b // per_dev, 2, at, :] = gv_v[b].astype(jnp.bfloat16)
            return carry

        lax.fori_loop(0, block_count, finish, 0)

    token_dims = (seq_devices, per_dev, quarters, rows, D_HEAD)
    out_dims = (seq_devices, 3, toks, D_HEAD)
    return pl.pallas_call(
        body,
        grid_spec=pltpu.PrefetchScalarGridSpec(
            num_scalar_prefetch=3,
            grid=(1,),
            in_specs=[pl.BlockSpec(memory_space=pl.ANY)] * (n_pieces + 1),
            out_specs=pl.BlockSpec(out_dims, lambda g, *s: (0, 0, 0, 0)),
            scratch_shapes=[
                pltpu.VMEM(token_dims, jnp.bfloat16),
                pltpu.VMEM(token_dims, jnp.bfloat16),
                pltpu.VMEM(token_dims, jnp.bfloat16),
                pltpu.VMEM((seq_devices, toks, D_HEAD), jnp.bfloat16),
                pltpu.VMEM((block_count, D_HEAD, BLOCK), jnp.bfloat16),
                pltpu.VMEM((block_count, BLOCK, D_HEAD), jnp.float32),
                pltpu.VMEM((block_count, BLOCK, D_HEAD), jnp.float32),
                pltpu.SemaphoreType.DMA((1 + 3 * n_pieces,)),
            ],
        ),
        out_shape=jax.ShapeDtypeStruct(out_dims, jnp.bfloat16),
        compiler_params=pltpu.CompilerParams(vmem_limit_bytes=40 << 20),
        cost_estimate=pl.CostEstimate(
            flops=40_000_000_000, transcendentals=0, bytes_accessed=64 << 20
        ),
        name=f"attention_{head}",
    )(tiles, counts, sources, *pieces, cot)


def unpack(head, arrived, outs, seq_devices):
    toks = arrived.shape[2]
    wide = HEADS_LOCAL * D_HEAD
    dims = (toks, seq_devices * wide)

    def body(src, *refs):
        dsts = refs[-4:-1]
        sem = refs[-1]
        copies = []
        for which in range(3):
            for dev in range(seq_devices):
                copies.append(
                    pltpu.make_async_copy(
                        src.at[dev, which],
                        dsts[which].at[:, pl.ds(dev * wide + head * D_HEAD, D_HEAD)],
                        sem.at[which * seq_devices + dev],
                    )
                )
        for copy in copies:
            copy.start()
        for copy in copies:
            copy.wait()

    return pl.pallas_call(
        body,
        in_specs=[pl.BlockSpec(memory_space=pltpu.VMEM)]
        + [pl.BlockSpec(memory_space=pl.ANY)] * len(outs),
        out_specs=[pl.BlockSpec(memory_space=pl.ANY)] * 3,
        out_shape=[jax.ShapeDtypeStruct(dims, jnp.bfloat16)] * 3,
        scratch_shapes=[pltpu.SemaphoreType.DMA((3 * seq_devices,))],
        input_output_aliases={1 + n: n for n in range(len(outs))},
        name=f"unpack_{head}",
    )(arrived, *outs)


def per_device(queries, keys, values, grad_out, table, positions, residues, tiles, counts):
    toks = queries.shape[0]
    row_devices = lax.axis_size("rows")
    seq_devices = lax.axis_size("seq")
    row = lax.axis_index("rows").astype(jnp.int32)
    first = lax.axis_index("seq").astype(jnp.int32) * toks
    chips = row_devices // 2
    spread = lambda x: lax.all_to_all(x, "seq", split_axis=0, concat_axis=0, tiled=True)

    def shift(x, hops):
        pairs = [
            (z * 2 + c, ((z + hops) % chips) * 2 + c) for z in range(chips) for c in range(2)
        ]
        return lax.ppermute(x, "rows", pairs)

    def swap(x):
        return lax.ppermute(x, "rows", [(n, n ^ 1) for n in range(row_devices)])

    own = spread(pack_inputs(row[None], queries, keys, values, row_devices, seq_devices))
    spot = jnp.stack([positions[0] - first, residues[0]])
    cots = pack_cotangent(spot, grad_out[0], table, seq_devices)
    cots = [spread(c) for c in cots]

    half = seq_devices // 2
    back, ahead = shift(own, 1), shift(own, -1)
    far_low, far_high = shift(back[:half], 1), shift(ahead[half:], -1)
    pieces = [own, back, ahead, far_low, far_high]
    spans = [(0, seq_devices)] * 3 + [(0, half), (half, seq_devices - half)]
    z, c = row // 2, row % 2
    steps = jnp.array([0, chips - 1, 1, 2, 2], jnp.int32)
    near = ((z + steps) % chips) * 2
    sources = jnp.concatenate([near + c, near + 1 - c])
    pieces = pieces + [swap(p) for p in pieces]
    spans = spans + spans

    outs = []
    for head in range(HEADS_LOCAL):
        grads = attention(
            head,
            tiles.reshape(-1),
            counts,
            sources,
            pieces,
            spans,
            cots[head],
            row_devices,
            seq_devices,
        )
        outs = unpack(head, spread(grads), outs, seq_devices)
    return tuple(x[None] for x in outs)


def solution(mesh):
    placed = (
        P("seq", None),
        P("seq", None),
        P("seq", None),
        P("rows", "seq", None),
        P(),
        P("rows"),
        P("rows"),
        P(),
        P(),
    )
    return jax.shard_map(
        per_device,
        mesh=mesh,
        in_specs=placed,
        out_specs=(P("rows", "seq", None), P("rows", "seq", None), P("rows", "seq", None)),
        check_vma=False,
    )
```

```python
import functools
import math

import jax
import jax.numpy as jnp
from jax import lax
from jax.experimental import pallas as pl
from jax.experimental.pallas import tpu as pltpu
from jax.sharding import PartitionSpec as P

D_HEAD = 128
BLOCK = 128
TILES = 8
HEADS_LOCAL = 2
SCALE = D_HEAD ** (-0.5)
EXP_SCALE = SCALE * math.log2(math.e)


def pack_first(shares, queries, keys, values, row_devices, seq_devices):
    toks, width = queries.shape
    rows = toks // row_devices
    wide = HEADS_LOCAL * D_HEAD

    def body(shares_ref, *refs):
        out_ref = refs[-1]
        for n, ref in enumerate(refs[:-1]):
            for dest in range(seq_devices):
                start = dest * wide
                out_ref[dest, n * rows : (n + 1) * rows] = ref[:, start : start + D_HEAD]

    near = pl.BlockSpec((rows, width), lambda g, shares_ref: (shares_ref[0], 0))
    far = pl.BlockSpec((rows, width), lambda g, shares_ref: (shares_ref[1], 0))
    out_dims = (seq_devices, 6 * rows, D_HEAD)
    return pl.pallas_call(
        body,
        grid_spec=pltpu.PrefetchScalarGridSpec(
            num_scalar_prefetch=1,
            grid=(1,),
            in_specs=[near, near, near, far, far, far],
            out_specs=pl.BlockSpec(out_dims, lambda g, shares_ref: (0, 0, 0)),
        ),
        out_shape=jax.ShapeDtypeStruct(out_dims, jnp.bfloat16),
        name="pack_first",
    )(shares, queries, keys, values, queries, keys, values)


def pack_rest(numbers, queries, keys, values, grad_out, table, row_devices, seq_devices):
    toks, width = grad_out.shape
    rows = toks // row_devices
    wide = HEADS_LOCAL * D_HEAD
    bases = (0, 6 * rows)

    def body(numbers_ref, *refs):
        share_refs = refs[:6]
        g_ref, table_ref = refs[6:8]
        outs = refs[8:]
        local = numbers_ref[2]
        residue = numbers_ref[3]
        for dest in range(seq_devices):
            for n, ref in enumerate(share_refs):
                start = dest * wide + D_HEAD
                outs[1][dest, n * rows : (n + 1) * rows] = ref[:, start : start + D_HEAD]
            for head in range(HEADS_LOCAL):
                start = dest * wide + head * D_HEAD
                outs[head][dest, bases[head] : bases[head] + toks] = g_ref[
                    :, start : start + D_HEAD
                ]

        @pl.when(jnp.logical_and(local >= 0, local < toks))
        def _():
            base = pl.multiple_of((local // 16) * 16, 16)
            picks = lax.broadcasted_iota(jnp.int32, (table.shape[0], D_HEAD), 0) == residue
            here = lax.broadcasted_iota(jnp.int32, (16, D_HEAD), 0) == local - base
            for dest in range(seq_devices):
                for head in range(HEADS_LOCAL):
                    start = dest * wide + head * D_HEAD
                    picked = table_ref[:, start : start + D_HEAD].astype(jnp.float32)
                    added = jnp.sum(jnp.where(picks, picked, 0.0), axis=0, keepdims=True)
                    now = g_ref[pl.ds(base, 16), start : start + D_HEAD].astype(jnp.float32)
                    outs[head][dest, pl.ds(pl.multiple_of(bases[head] + base, 16), 16), :] = (
                        now + jnp.where(here, added, 0.0)
                    ).astype(jnp.bfloat16)

    near = pl.BlockSpec((rows, width), lambda g, numbers_ref: (numbers_ref[0], 0))
    far = pl.BlockSpec((rows, width), lambda g, numbers_ref: (numbers_ref[1], 0))
    dims = [(seq_devices, base + toks, D_HEAD) for base in bases]
    return pl.pallas_call(
        body,
        grid_spec=pltpu.PrefetchScalarGridSpec(
            num_scalar_prefetch=1,
            grid=(1,),
            in_specs=[near, near, near, far, far, far]
            + [
                pl.BlockSpec((toks, width), lambda g, s: (0, 0)),
                pl.BlockSpec(table.shape, lambda g, s: (0, 0)),
            ],
            out_specs=[pl.BlockSpec(d, lambda g, s: (0, 0, 0)) for d in dims],
        ),
        out_shape=[jax.ShapeDtypeStruct(d, jnp.bfloat16) for d in dims],
        cost_estimate=pl.CostEstimate(
            flops=5_000_000_000, transcendentals=0, bytes_accessed=4 * toks * width
        ),
        name="pack_rest",
    )(numbers, queries, keys, values, queries, keys, values, grad_out, table)


def dot_nt(left, right):
    return lax.dot_general(left, right, (((1,), (1,)), ((), ())), preferred_element_type=jnp.float32)


def dot_nn(left, right):
    return lax.dot_general(left, right, (((1,), (0,)), ((), ())), preferred_element_type=jnp.float32)


def attention(head, tiles, counts, order, sources, arrays, parts, cot, toks, row_devices):
    seq_devices = arrays[0].shape[0]
    rows = toks // row_devices
    block_count = seq_devices * toks // BLOCK
    per_dev = toks // BLOCK
    quarters = BLOCK // rows
    n_arrays = len(arrays)
    n_in = 1 + 3 * row_devices
    many = 4

    def body(tiles_ref, counts_ref, order_ref, source_ref, *refs):
        array_refs = refs[:n_arrays]
        out_hbm = refs[n_arrays]
        q_v, kv_v, c_v, kt_v, grads_v, out_ref, even_s, odd_s, even_t, odd_t, sem = refs[
            n_arrays + 1 :
        ]
        found_v, terms_v = (even_s, odd_s), (even_t, odd_t)
        lanes = (None, pl.ds(0, D_HEAD), pl.ds(D_HEAD, D_HEAD))
        copies = []
        for p, (which_array, begin_row) in enumerate(parts):
            share = source_ref[p]
            for which in range(3):
                if which == 0:
                    dst = q_v.at[:, share // quarters, share % quarters]
                else:
                    dst = kv_v.at[:, share // quarters, share % quarters, :, lanes[which]]
                src = array_refs[which_array].at[:, pl.ds(begin_row + which * rows, rows)]
                copies.append(pltpu.make_async_copy(src, dst, sem.at[3 * p + which]))
        copies.append(
            pltpu.make_async_copy(
                array_refs[cot[0]].at[:, pl.ds(cot[1], toks)], c_v, sem.at[n_in - 1]
            )
        )
        for copy in copies:
            copy.start()

        def clear(b, carry):
            grads_v[b] = jnp.zeros((BLOCK, 2 * D_HEAD), jnp.float32)
            return carry

        for ref in found_v + terms_v:
            ref[...] = jnp.zeros(ref.shape, ref.dtype)

        lax.fori_loop(0, block_count, clear, 0)
        for copy in copies:
            copy.wait()

        def flip(g, carry):
            for n in range(many):
                b = g * many + n
                block = kv_v[b // per_dev, b % per_dev, :, :, :D_HEAD]
                kt_v[b] = block.reshape(BLOCK, D_HEAD).T
            return carry

        lax.fori_loop(0, block_count // many, flip, 0)

        def at_block(b):
            return pl.ds(pl.multiple_of((b % per_dev) * BLOCK, BLOCK), BLOCK)

        def tile_of(i, j):
            return jnp.where(j < counts_ref[i], tiles_ref[i * TILES + j], i)

        def begin(i, count, found_ref):
            q_b = q_v[i // per_dev, i % per_dev].reshape(BLOCK, D_HEAD)
            c_b = c_v[i // per_dev, at_block(i), :]
            ids = [tile_of(i, j) for j in range(count)]
            blocks = [kv_v[t // per_dev, t % per_dev] for t in ids]
            k_all = jnp.concatenate(
                [x[:, :, :D_HEAD].reshape(BLOCK, D_HEAD) for x in blocks], axis=0
            )
            v_all = jnp.concatenate(
                [x[:, :, D_HEAD:].reshape(BLOCK, D_HEAD) for x in blocks], axis=0
            )
            found_ref[: count * BLOCK, :D_HEAD] = dot_nt(k_all, q_b)
            found_ref[: count * BLOCK, D_HEAD:] = dot_nt(v_all, c_b)

        def middle(used, count, found_ref, terms_ref):
            cuts = [slice(j * BLOCK, (j + 1) * BLOCK) for j in range(count)]
            tops = [
                jnp.where(j < used, jnp.max(found_ref[c, :D_HEAD], axis=0, keepdims=True), -jnp.inf)
                for j, c in enumerate(cuts)
            ]
            top = functools.reduce(jnp.maximum, tops) * EXP_SCALE
            total, delta, probs = 0.0, 0.0, []
            for j, c in enumerate(cuts):
                shift = jnp.where(j < used, top, jnp.inf)
                p = jnp.exp2(found_ref[c, :D_HEAD] * EXP_SCALE - shift)
                total = total + p
                delta = delta + p * found_ref[c, D_HEAD:]
                probs.append(p)
            total = jnp.sum(total, axis=0, keepdims=True)
            inverse = jnp.where(used > 0, 1.0 / total, 0.0)
            delta = jnp.sum(delta, axis=0, keepdims=True) * inverse
            for c, p in zip(cuts, probs):
                p = p * inverse
                terms_ref[c, :D_HEAD] = (p * (found_ref[c, D_HEAD:] - delta)).astype(jnp.bfloat16)
                terms_ref[c, D_HEAD:] = p.astype(jnp.bfloat16)

        def end(i, count, terms_ref):
            q_b = q_v[i // per_dev, i % per_dev].reshape(BLOCK, D_HEAD)
            c_b = c_v[i // per_dev, at_block(i), :]
            ids = [tile_of(i, j) for j in range(count)]
            scores = terms_ref[: count * BLOCK, :D_HEAD]
            probs = terms_ref[: count * BLOCK, D_HEAD:]
            key_terms = dot_nn(scores, q_b)
            value_terms = dot_nn(probs, c_b)
            grad_q = dot_nn(jnp.concatenate([kt_v[t] for t in ids], axis=1), scores)
            for j, t in enumerate(ids):
                grads_v[t, :, :D_HEAD] += key_terms[j * BLOCK : (j + 1) * BLOCK]
                grads_v[t, :, D_HEAD:] += value_terms[j * BLOCK : (j + 1) * BLOCK]
            out_ref[i // per_dev, 0, at_block(i), :] = (grad_q.T * SCALE).astype(jnp.bfloat16)

        def step(half, carry):
            for parity in range(2):
                g = 2 * half + parity
                first = order_ref[jnp.minimum(g, block_count - 1)]
                second = order_ref[jnp.clip(g - 1, 0, block_count - 1)]
                third = order_ref[jnp.maximum(g - 2, 0)]
                used = jnp.where(g > 0, counts_ref[second], 0)
                most = counts_ref[third]

                def choose(low, high, first, second, third, used, most, parity):
                    if low == high:
                        end(third, low, terms_v[parity])
                        middle(used, low, found_v[1 - parity], terms_v[1 - parity])
                        begin(first, low, found_v[parity])
                        return
                    split = (low + high) // 2

                    @pl.when(most <= split)
                    def _():
                        choose(low, split, first, second, third, used, most, parity)

                    @pl.when(most > split)
                    def _():
                        choose(split + 1, high, first, second, third, used, most, parity)

                choose(1, TILES, first, second, third, used, most, parity)

            return carry

        lax.fori_loop(0, block_count // 2 + 1, step, 0)

        stored = [pltpu.make_async_copy(out_ref.at[:, 0], out_hbm.at[:, 0], sem.at[n_in])]
        stored[0].start()
        quarter = seq_devices // many
        for part in range(many):

            def finish(dev, carry):
                for n in range(per_dev):
                    grads = grads_v[dev * per_dev + n]
                    at = pl.ds(n * BLOCK, BLOCK)
                    out_ref[dev, 1, at, :] = (grads[:, :D_HEAD] * SCALE).astype(jnp.bfloat16)
                    out_ref[dev, 2, at, :] = grads[:, D_HEAD:].astype(jnp.bfloat16)
                return carry

            lax.fori_loop(part * quarter, (part + 1) * quarter, finish, 0)
            at = (pl.ds(part * quarter, quarter), pl.ds(1, 2))
            stored.append(
                pltpu.make_async_copy(out_ref.at[at], out_hbm.at[at], sem.at[n_in + 1 + part])
            )
            stored[-1].start()
        for copy in stored:
            copy.wait()

    token_dims = (seq_devices, per_dev, quarters, rows)
    out_dims = (seq_devices, 3, toks, D_HEAD)
    return pl.pallas_call(
        body,
        grid_spec=pltpu.PrefetchScalarGridSpec(
            num_scalar_prefetch=4,
            grid=(1,),
            in_specs=[pl.BlockSpec(memory_space=pl.ANY)] * n_arrays,
            out_specs=pl.BlockSpec(memory_space=pltpu.HBM),
            scratch_shapes=[
                pltpu.VMEM(token_dims + (D_HEAD,), jnp.bfloat16),
                pltpu.VMEM(token_dims + (2 * D_HEAD,), jnp.bfloat16),
                pltpu.VMEM((seq_devices, toks, D_HEAD), jnp.bfloat16),
                pltpu.VMEM((block_count, D_HEAD, BLOCK), jnp.bfloat16),
                pltpu.VMEM((block_count, BLOCK, 2 * D_HEAD), jnp.float32),
                pltpu.VMEM(out_dims, jnp.bfloat16),
                pltpu.VMEM((TILES * BLOCK, 2 * D_HEAD), jnp.float32),
                pltpu.VMEM((TILES * BLOCK, 2 * D_HEAD), jnp.float32),
                pltpu.VMEM((TILES * BLOCK, 2 * D_HEAD), jnp.bfloat16),
                pltpu.VMEM((TILES * BLOCK, 2 * D_HEAD), jnp.bfloat16),
                pltpu.SemaphoreType.DMA((n_in + 1 + many,)),
            ],
        ),
        out_shape=jax.ShapeDtypeStruct(out_dims, jnp.bfloat16),
        compiler_params=pltpu.CompilerParams(vmem_limit_bytes=60 << 20),
        cost_estimate=pl.CostEstimate(
            flops=(40_000_000_000, 1_000_000)[head], transcendentals=0, bytes_accessed=1 << 20
        ),
        name=f"attention_{head}",
    )(tiles, counts, order, sources, *arrays)


def unpack(head, arrived, outs, seq_devices):
    toks = arrived.shape[2]
    wide = HEADS_LOCAL * D_HEAD
    dims = (toks, seq_devices * wide)

    def body(src, *refs):
        dsts = refs[-4:-1]
        sem = refs[-1]
        copies = []
        for which in range(3):
            for dev in range(seq_devices):
                copies.append(
                    pltpu.make_async_copy(
                        src.at[dev, which],
                        dsts[which].at[:, pl.ds(dev * wide + head * D_HEAD, D_HEAD)],
                        sem.at[which * seq_devices + dev],
                    )
                )
        for copy in copies:
            copy.start()
        for copy in copies:
            copy.wait()

    return pl.pallas_call(
        body,
        in_specs=[pl.BlockSpec(memory_space=pltpu.VMEM)]
        + [pl.BlockSpec(memory_space=pl.ANY)] * len(outs),
        out_specs=[pl.BlockSpec(memory_space=pl.ANY)] * 3,
        out_shape=[jax.ShapeDtypeStruct(dims, jnp.bfloat16)] * 3,
        scratch_shapes=[pltpu.SemaphoreType.DMA((3 * seq_devices,))],
        input_output_aliases={1 + n: n for n in range(len(outs))},
        name=f"unpack_{head}",
    )(arrived, *outs)


def per_device(queries, keys, values, grad_out, table, positions, residues, tiles, counts):
    toks = queries.shape[0]
    row_devices = lax.axis_size("rows")
    seq_devices = lax.axis_size("seq")
    row = lax.axis_index("rows").astype(jnp.int32)
    first = lax.axis_index("seq").astype(jnp.int32) * toks
    chips = row_devices // 2
    spread = lambda x: lax.all_to_all(x, "seq", split_axis=0, concat_axis=0, tiled=True)

    def shift(x, hops):
        pairs = [
            (z * 2 + c, ((z + hops) % chips) * 2 + c) for z in range(chips) for c in range(2)
        ]
        return lax.ppermute(x, "rows", pairs)

    def swap(x):
        return lax.ppermute(x, "rows", [(n, n ^ 1) for n in range(row_devices)])

    half = row_devices // 2
    rows = toks // row_devices
    numbers = jnp.stack([row, (row + half) % row_devices, positions[0] - first, residues[0]])
    own = pack_first(numbers, queries, keys, values, row_devices, seq_devices)
    cot, late = pack_rest(
        numbers, queries, keys, values, grad_out[0], table, row_devices, seq_devices
    )
    own = spread(own)
    sources = jnp.stack(
        [row, row + half, row ^ 1, (row ^ 1) + half, row - 2, row + 2, (row ^ 1) - 2, (row ^ 1) + 2]
    )
    sources = sources % row_devices

    blocks = jnp.arange(counts.shape[0], dtype=jnp.int32)
    ahead_of = (counts[None, :] > counts[:, None]) | (
        (counts[None, :] == counts[:, None]) & (blocks[None, :] < blocks[:, None])
    )
    place = jnp.sum(ahead_of.astype(jnp.int32), axis=1)
    order = jnp.sum(jnp.where(place[None, :] == blocks[:, None], blocks[None, :], 0), axis=1)

    def gather(near):
        back, ahead = shift(near, 1), shift(near, -1)
        return [back, ahead, swap(back), swap(ahead)]

    def work(head, arrays, cot_at):
        parts = [(0, 0), (0, 3 * rows), (1, 0), (1, 3 * rows), (2, 0), (3, 0), (4, 0), (5, 0)]
        return attention(
            head,
            tiles.reshape(-1),
            counts,
            order,
            sources,
            arrays,
            parts,
            cot_at,
            toks,
            row_devices,
        )

    own, cot, late = lax.optimization_barrier((own, cot, late))
    near = own[:, : 3 * rows]
    arrays = [own, swap(own)] + gather(near)
    cot = spread(cot)
    cot, late = lax.optimization_barrier((cot, late))
    late = spread(late)
    grads = work(0, arrays + [cot], (6, 0))
    grads, late = lax.optimization_barrier((grads, late))
    first_out = spread(grads)
    arrays = [late, swap(late[:, : 6 * rows])] + gather(late[:, : 3 * rows])
    grads = work(1, arrays, (0, 6 * rows))
    outs = unpack(0, first_out, [], seq_devices)
    outs = unpack(1, spread(grads), outs, seq_devices)
    return tuple(x[None] for x in outs)


def solution(mesh):
    placed = (
        P("seq", None),
        P("seq", None),
        P("seq", None),
        P("rows", "seq", None),
        P(),
        P("rows"),
        P("rows"),
        P(),
        P(),
    )
    return jax.shard_map(
        per_device,
        mesh=mesh,
        in_specs=placed,
        out_specs=(P("rows", "seq", None), P("rows", "seq", None), P("rows", "seq", None)),
        check_vma=False,
    )
```

```python
import functools
import math

import jax
import jax.numpy as jnp
from jax import lax
from jax.experimental import pallas as pl
from jax.experimental.pallas import tpu as pltpu
from jax.sharding import PartitionSpec as P

D_HEAD = 128
BLOCK = 128
TILES = 8
HEADS_LOCAL = 2
SCALE = D_HEAD ** (-0.5)
EXP_SCALE = SCALE * math.log2(math.e)


def pack_first(shares, queries, keys, values, row_devices, seq_devices):
    toks, width = queries.shape
    rows = toks // row_devices
    wide = HEADS_LOCAL * D_HEAD

    def body(shares_ref, *refs):
        out_ref = refs[-1]
        for n, ref in enumerate(refs[:-1]):
            for dest in range(seq_devices):
                start = dest * wide
                out_ref[dest, n * rows : (n + 1) * rows] = ref[:, start : start + D_HEAD]

    near = pl.BlockSpec((rows, width), lambda g, shares_ref: (shares_ref[0], 0))
    far = pl.BlockSpec((rows, width), lambda g, shares_ref: (shares_ref[1], 0))
    out_dims = (seq_devices, 6 * rows, D_HEAD)
    return pl.pallas_call(
        body,
        grid_spec=pltpu.PrefetchScalarGridSpec(
            num_scalar_prefetch=1,
            grid=(1,),
            in_specs=[near, near, near, far, far, far],
            out_specs=pl.BlockSpec(out_dims, lambda g, shares_ref: (0, 0, 0)),
        ),
        out_shape=jax.ShapeDtypeStruct(out_dims, jnp.bfloat16),
        name="pack_first",
    )(shares, queries, keys, values, queries, keys, values)


def pack_rest(numbers, queries, keys, values, grad_out, table, row_devices, seq_devices):
    toks, width = grad_out.shape
    rows = toks // row_devices
    wide = HEADS_LOCAL * D_HEAD
    bases = (0, 6 * rows)

    def body(numbers_ref, *refs):
        share_refs = refs[:6]
        g_ref, table_ref = refs[6:8]
        outs = refs[8:]
        local = numbers_ref[2]
        residue = numbers_ref[3]
        for dest in range(seq_devices):
            for n, ref in enumerate(share_refs):
                start = dest * wide + D_HEAD
                outs[1][dest, n * rows : (n + 1) * rows] = ref[:, start : start + D_HEAD]
            for head in range(HEADS_LOCAL):
                start = dest * wide + head * D_HEAD
                outs[head][dest, bases[head] : bases[head] + toks] = g_ref[
                    :, start : start + D_HEAD
                ]

        @pl.when(jnp.logical_and(local >= 0, local < toks))
        def _():
            base = pl.multiple_of((local // 16) * 16, 16)
            picks = lax.broadcasted_iota(jnp.int32, (table.shape[0], D_HEAD), 0) == residue
            here = lax.broadcasted_iota(jnp.int32, (16, D_HEAD), 0) == local - base
            for dest in range(seq_devices):
                for head in range(HEADS_LOCAL):
                    start = dest * wide + head * D_HEAD
                    picked = table_ref[:, start : start + D_HEAD].astype(jnp.float32)
                    added = jnp.sum(jnp.where(picks, picked, 0.0), axis=0, keepdims=True)
                    now = g_ref[pl.ds(base, 16), start : start + D_HEAD].astype(jnp.float32)
                    outs[head][dest, pl.ds(pl.multiple_of(bases[head] + base, 16), 16), :] = (
                        now + jnp.where(here, added, 0.0)
                    ).astype(jnp.bfloat16)

    near = pl.BlockSpec((rows, width), lambda g, numbers_ref: (numbers_ref[0], 0))
    far = pl.BlockSpec((rows, width), lambda g, numbers_ref: (numbers_ref[1], 0))
    dims = [(seq_devices, base + toks, D_HEAD) for base in bases]
    return pl.pallas_call(
        body,
        grid_spec=pltpu.PrefetchScalarGridSpec(
            num_scalar_prefetch=1,
            grid=(1,),
            in_specs=[near, near, near, far, far, far]
            + [
                pl.BlockSpec((toks, width), lambda g, s: (0, 0)),
                pl.BlockSpec(table.shape, lambda g, s: (0, 0)),
            ],
            out_specs=[pl.BlockSpec(d, lambda g, s: (0, 0, 0)) for d in dims],
        ),
        out_shape=[jax.ShapeDtypeStruct(d, jnp.bfloat16) for d in dims],
        cost_estimate=pl.CostEstimate(
            flops=5_000_000_000, transcendentals=0, bytes_accessed=4 * toks * width
        ),
        name="pack_rest",
    )(numbers, queries, keys, values, queries, keys, values, grad_out, table)


def dot_nt(left, right):
    return lax.dot_general(left, right, (((1,), (1,)), ((), ())), preferred_element_type=jnp.float32)


def dot_nn(left, right):
    return lax.dot_general(left, right, (((1,), (0,)), ((), ())), preferred_element_type=jnp.float32)


def attention(head, tiles, counts, order, sources, arrays, parts, cot, toks, row_devices):
    seq_devices = arrays[0].shape[0]
    rows = toks // row_devices
    block_count = seq_devices * toks // BLOCK
    per_dev = toks // BLOCK
    quarters = BLOCK // rows
    n_arrays = len(arrays)
    n_in = 1 + 3 * row_devices
    many = 4

    def body(tiles_ref, counts_ref, order_ref, source_ref, *refs):
        array_refs = refs[:n_arrays]
        out_hbm = refs[n_arrays]
        q_v, kv_v, c_v, kt_v, grads_v, out_ref, even_s, odd_s, even_t, odd_t, sem = refs[
            n_arrays + 1 :
        ]
        found_v, terms_v = (even_s, odd_s), (even_t, odd_t)
        lanes = (None, pl.ds(0, D_HEAD), pl.ds(D_HEAD, D_HEAD))
        copies = []
        for p, (which_array, begin_row) in enumerate(parts):
            share = source_ref[p]
            for which in range(3):
                if which == 0:
                    dst = q_v.at[:, share // quarters, share % quarters]
                else:
                    dst = kv_v.at[:, share // quarters, share % quarters, :, lanes[which]]
                src = array_refs[which_array].at[:, pl.ds(begin_row + which * rows, rows)]
                copies.append(pltpu.make_async_copy(src, dst, sem.at[3 * p + which]))
        copies.append(
            pltpu.make_async_copy(
                array_refs[cot[0]].at[:, pl.ds(cot[1], toks)], c_v, sem.at[n_in - 1]
            )
        )
        for copy in copies:
            copy.start()

        def clear(b, carry):
            grads_v[b] = jnp.zeros((BLOCK, 2 * D_HEAD), jnp.float32)
            return carry

        for ref in found_v + terms_v:
            ref[...] = jnp.zeros(ref.shape, ref.dtype)

        lax.fori_loop(0, block_count, clear, 0)
        for copy in copies:
            copy.wait()

        def flip(g, carry):
            for n in range(many):
                b = g * many + n
                block = kv_v[b // per_dev, b % per_dev, :, :, :D_HEAD]
                kt_v[b] = block.reshape(BLOCK, D_HEAD).T
            return carry

        lax.fori_loop(0, block_count // many, flip, 0)

        def at_block(b):
            return pl.ds(pl.multiple_of((b % per_dev) * BLOCK, BLOCK), BLOCK)

        def tile_of(i, j):
            return jnp.where(j < counts_ref[i], tiles_ref[i * TILES + j], i)

        def begin(i, count, found_ref):
            q_b = q_v[i // per_dev, i % per_dev].reshape(BLOCK, D_HEAD)
            c_b = c_v[i // per_dev, at_block(i), :]
            ids = [tile_of(i, j) for j in range(count)]
            blocks = [kv_v[t // per_dev, t % per_dev] for t in ids]
            k_all = jnp.concatenate(
                [x[:, :, :D_HEAD].reshape(BLOCK, D_HEAD) for x in blocks], axis=0
            )
            v_all = jnp.concatenate(
                [x[:, :, D_HEAD:].reshape(BLOCK, D_HEAD) for x in blocks], axis=0
            )
            found_ref[: count * BLOCK, :D_HEAD] = dot_nt(k_all, q_b)
            found_ref[: count * BLOCK, D_HEAD:] = dot_nt(v_all, c_b)

        def middle(used, count, found_ref, terms_ref):
            cuts = [slice(j * BLOCK, (j + 1) * BLOCK) for j in range(count)]
            tops = [
                jnp.where(j < used, jnp.max(found_ref[c, :D_HEAD], axis=0, keepdims=True), -jnp.inf)
                for j, c in enumerate(cuts)
            ]
            top = functools.reduce(jnp.maximum, tops) * EXP_SCALE
            total, delta, probs = 0.0, 0.0, []
            for j, c in enumerate(cuts):
                shift = jnp.where(j < used, top, jnp.inf)
                p = jnp.exp2(found_ref[c, :D_HEAD] * EXP_SCALE - shift)
                total = total + p
                delta = delta + p * found_ref[c, D_HEAD:]
                probs.append(p)
            total = jnp.sum(total, axis=0, keepdims=True)
            inverse = jnp.where(used > 0, 1.0 / total, 0.0)
            delta = jnp.sum(delta, axis=0, keepdims=True) * inverse
            for c, p in zip(cuts, probs):
                p = p * inverse
                terms_ref[c, :D_HEAD] = (p * (found_ref[c, D_HEAD:] - delta)).astype(jnp.bfloat16)
                terms_ref[c, D_HEAD:] = p.astype(jnp.bfloat16)

        def end(i, count, terms_ref):
            q_b = q_v[i // per_dev, i % per_dev].reshape(BLOCK, D_HEAD)
            c_b = c_v[i // per_dev, at_block(i), :]
            ids = [tile_of(i, j) for j in range(count)]
            scores = terms_ref[: count * BLOCK, :D_HEAD]
            probs = terms_ref[: count * BLOCK, D_HEAD:]
            key_terms = dot_nn(scores, q_b)
            value_terms = dot_nn(probs, c_b)
            grad_q = dot_nn(jnp.concatenate([kt_v[t] for t in ids], axis=1), scores)
            for j, t in enumerate(ids):
                grads_v[t, :, :D_HEAD] += key_terms[j * BLOCK : (j + 1) * BLOCK]
                grads_v[t, :, D_HEAD:] += value_terms[j * BLOCK : (j + 1) * BLOCK]
            out_ref[i // per_dev, 0, at_block(i), :] = (grad_q.T * SCALE).astype(jnp.bfloat16)

        def step(half, carry):
            for parity in range(2):
                g = 2 * half + parity
                first = order_ref[jnp.minimum(g, block_count - 1)]
                second = order_ref[jnp.clip(g - 1, 0, block_count - 1)]
                third = order_ref[jnp.maximum(g - 2, 0)]
                used = jnp.where(g > 0, counts_ref[second], 0)
                most = counts_ref[third]

                def choose(low, high, first, second, third, used, most, parity):
                    if low == high:
                        end(third, low, terms_v[parity])
                        middle(used, low, found_v[1 - parity], terms_v[1 - parity])
                        begin(first, low, found_v[parity])
                        return
                    split = (low + high) // 2

                    @pl.when(most <= split)
                    def _():
                        choose(low, split, first, second, third, used, most, parity)

                    @pl.when(most > split)
                    def _():
                        choose(split + 1, high, first, second, third, used, most, parity)

                choose(1, TILES, first, second, third, used, most, parity)

            return carry

        lax.fori_loop(0, block_count // 2 + 1, step, 0)

        stored = [pltpu.make_async_copy(out_ref.at[:, 0], out_hbm.at[:, 0], sem.at[n_in])]
        stored[0].start()
        quarter = seq_devices // many
        for part in range(many):

            def finish(dev, carry):
                for n in range(per_dev):
                    grads = grads_v[dev * per_dev + n]
                    at = pl.ds(n * BLOCK, BLOCK)
                    out_ref[dev, 1, at, :] = (grads[:, :D_HEAD] * SCALE).astype(jnp.bfloat16)
                    out_ref[dev, 2, at, :] = grads[:, D_HEAD:].astype(jnp.bfloat16)
                return carry

            lax.fori_loop(part * quarter, (part + 1) * quarter, finish, 0)
            at = (pl.ds(part * quarter, quarter), pl.ds(1, 2))
            stored.append(
                pltpu.make_async_copy(out_ref.at[at], out_hbm.at[at], sem.at[n_in + 1 + part])
            )
            stored[-1].start()
        for copy in stored:
            copy.wait()

    token_dims = (seq_devices, per_dev, quarters, rows)
    out_dims = (seq_devices, 3, toks, D_HEAD)
    return pl.pallas_call(
        body,
        grid_spec=pltpu.PrefetchScalarGridSpec(
            num_scalar_prefetch=4,
            grid=(1,),
            in_specs=[pl.BlockSpec(memory_space=pl.ANY)] * n_arrays,
            out_specs=pl.BlockSpec(memory_space=pltpu.HBM),
            scratch_shapes=[
                pltpu.VMEM(token_dims + (D_HEAD,), jnp.bfloat16),
                pltpu.VMEM(token_dims + (2 * D_HEAD,), jnp.bfloat16),
                pltpu.VMEM((seq_devices, toks, D_HEAD), jnp.bfloat16),
                pltpu.VMEM((block_count, D_HEAD, BLOCK), jnp.bfloat16),
                pltpu.VMEM((block_count, BLOCK, 2 * D_HEAD), jnp.float32),
                pltpu.VMEM(out_dims, jnp.bfloat16),
                pltpu.VMEM((TILES * BLOCK, 2 * D_HEAD), jnp.float32),
                pltpu.VMEM((TILES * BLOCK, 2 * D_HEAD), jnp.float32),
                pltpu.VMEM((TILES * BLOCK, 2 * D_HEAD), jnp.bfloat16),
                pltpu.VMEM((TILES * BLOCK, 2 * D_HEAD), jnp.bfloat16),
                pltpu.SemaphoreType.DMA((n_in + 1 + many,)),
            ],
        ),
        out_shape=pltpu.HBM(out_dims, jnp.bfloat16),
        compiler_params=pltpu.CompilerParams(vmem_limit_bytes=32 << 20),
        cost_estimate=pl.CostEstimate(
            flops=(40_000_000_000, 1_000_000)[head], transcendentals=0, bytes_accessed=1 << 20
        ),
        name=f"attention_{head}",
    )(tiles, counts, order, sources, *arrays)


def unpack(head, arrived, outs, seq_devices):
    toks = arrived.shape[2]
    wide = HEADS_LOCAL * D_HEAD
    dims = (toks, seq_devices * wide)

    def body(src, *refs):
        dsts = refs[-4:-1]
        sem = refs[-1]
        copies = []
        for which in range(3):
            for dev in range(seq_devices):
                copies.append(
                    pltpu.make_async_copy(
                        src.at[dev, which],
                        dsts[which].at[:, pl.ds(dev * wide + head * D_HEAD, D_HEAD)],
                        sem.at[which * seq_devices + dev],
                    )
                )
        for copy in copies:
            copy.start()
        for copy in copies:
            copy.wait()

    return pl.pallas_call(
        body,
        in_specs=[pl.BlockSpec(memory_space=pl.ANY if outs else pltpu.VMEM)]
        + [pl.BlockSpec(memory_space=pl.ANY)] * len(outs),
        out_specs=[pl.BlockSpec(memory_space=pl.ANY)] * 3,
        out_shape=[jax.ShapeDtypeStruct(dims, jnp.bfloat16)] * 3,
        scratch_shapes=[pltpu.SemaphoreType.DMA((3 * seq_devices,))],
        input_output_aliases={1 + n: n for n in range(len(outs))},
        compiler_params=pltpu.CompilerParams(vmem_limit_bytes=8 << 20),
        name=f"unpack_{head}",
    )(arrived, *outs)


def per_device(queries, keys, values, grad_out, table, positions, residues, tiles, counts):
    toks = queries.shape[0]
    row_devices = lax.axis_size("rows")
    seq_devices = lax.axis_size("seq")
    row = lax.axis_index("rows").astype(jnp.int32)
    first = lax.axis_index("seq").astype(jnp.int32) * toks
    chips = row_devices // 2
    spread = lambda x: lax.all_to_all(x, "seq", split_axis=0, concat_axis=0, tiled=True)

    def shift(x, hops):
        pairs = [
            (z * 2 + c, ((z + hops) % chips) * 2 + c) for z in range(chips) for c in range(2)
        ]
        return lax.ppermute(x, "rows", pairs)

    def swap(x):
        return lax.ppermute(x, "rows", [(n, n ^ 1) for n in range(row_devices)])

    half = row_devices // 2
    rows = toks // row_devices
    shares = jnp.stack([row, (row + half) % row_devices])
    numbers = jnp.stack([row, (row + half) % row_devices, positions[0] - first, residues[0]])
    own = pack_first(shares, queries, keys, values, row_devices, seq_devices)
    cot, late = pack_rest(
        numbers, queries, keys, values, grad_out[0], table, row_devices, seq_devices
    )
    own = spread(own)
    sources = jnp.stack(
        [row, row + half, row ^ 1, (row ^ 1) + half, row - 2, row + 2, (row ^ 1) - 2, (row ^ 1) + 2]
    )
    sources = sources % row_devices

    blocks = jnp.arange(counts.shape[0], dtype=jnp.int32)
    ahead_of = (counts[None, :] > counts[:, None]) | (
        (counts[None, :] == counts[:, None]) & (blocks[None, :] < blocks[:, None])
    )
    place = jnp.sum(ahead_of.astype(jnp.int32), axis=1)
    order = jnp.sum(jnp.where(place[None, :] == blocks[:, None], blocks[None, :], 0), axis=1)

    def gather(near):
        back, ahead = shift(near, 1), shift(near, -1)
        return [back, ahead, swap(back), swap(ahead)]

    def work(head, arrays, cot_at):
        parts = [(0, 0), (0, 3 * rows), (1, 0), (1, 3 * rows), (2, 0), (3, 0), (4, 0), (5, 0)]
        return attention(
            head,
            tiles.reshape(-1),
            counts,
            order,
            sources,
            arrays,
            parts,
            cot_at,
            toks,
            row_devices,
        )

    own, cot, late = lax.optimization_barrier((own, cot, late))
    near = own[:, : 3 * rows]
    arrays = [own, swap(own)] + gather(near)
    cot = spread(cot)
    cot, late = lax.optimization_barrier((cot, late))
    late = spread(late)
    grads = work(0, arrays + [cot], (6, 0))
    grads, late = lax.optimization_barrier((grads, late))
    first_out = spread(grads)
    arrays = [late, swap(late[:, : 6 * rows])] + gather(late[:, : 3 * rows])
    grads = work(1, arrays, (0, 6 * rows))
    outs = unpack(0, first_out, [], seq_devices)
    outs = unpack(1, spread(grads), outs, seq_devices)
    return tuple(x[None] for x in outs)


def solution(mesh):
    placed = (
        P("seq", None),
        P("seq", None),
        P("seq", None),
        P("rows", "seq", None),
        P(),
        P("rows"),
        P("rows"),
        P(),
        P(),
    )
    return jax.shard_map(
        per_device,
        mesh=mesh,
        in_specs=placed,
        out_specs=(P("rows", "seq", None), P("rows", "seq", None), P("rows", "seq", None)),
        check_vma=False,
    )
```

```python
import functools
import math

import jax
import jax.numpy as jnp
from jax import lax
from jax.experimental import pallas as pl
from jax.experimental.pallas import tpu as pltpu
from jax.sharding import PartitionSpec as P

D_HEAD = 128
BLOCK = 128
TILES = 8
HEADS_LOCAL = 2
SCALE = D_HEAD ** (-0.5)
EXP_SCALE = SCALE * math.log2(math.e)


def pack_first(share, queries, keys, values, row_devices, seq_devices):
    toks, width = queries.shape
    rows = toks // row_devices
    wide = HEADS_LOCAL * D_HEAD

    def body(share_ref, *refs):
        out_ref = refs[-1]
        for n, ref in enumerate(refs[:-1]):
            for dest in range(seq_devices):
                start = dest * wide
                out_ref[dest, n * rows : (n + 1) * rows] = ref[:, start : start + D_HEAD]

    near = pl.BlockSpec((rows, width), lambda g, share_ref: (share_ref[0], 0))
    out_dims = (seq_devices, 3 * rows, D_HEAD)
    return pl.pallas_call(
        body,
        grid_spec=pltpu.PrefetchScalarGridSpec(
            num_scalar_prefetch=1,
            grid=(1,),
            in_specs=[near, near, near],
            out_specs=pl.BlockSpec(out_dims, lambda g, share_ref: (0, 0, 0)),
        ),
        out_shape=jax.ShapeDtypeStruct(out_dims, jnp.bfloat16),
        name="pack_first",
    )(share, queries, keys, values)


def pack_rest(numbers, queries, keys, values, grad_out, table, row_devices, seq_devices):
    toks, width = grad_out.shape
    rows = toks // row_devices
    wide = HEADS_LOCAL * D_HEAD
    bases = (0, 6 * rows)

    def body(numbers_ref, *refs):
        share_refs = refs[:6]
        g_ref, table_ref = refs[6:8]
        outs = refs[8:]
        local = numbers_ref[2]
        residue = numbers_ref[3]
        for dest in range(seq_devices):
            for n, ref in enumerate(share_refs):
                start = dest * wide + D_HEAD
                outs[1][dest, n * rows : (n + 1) * rows] = ref[:, start : start + D_HEAD]
            for head in range(HEADS_LOCAL):
                start = dest * wide + head * D_HEAD
                outs[head][dest, bases[head] : bases[head] + toks] = g_ref[
                    :, start : start + D_HEAD
                ]

        @pl.when(jnp.logical_and(local >= 0, local < toks))
        def _():
            base = pl.multiple_of((local // 16) * 16, 16)
            picks = lax.broadcasted_iota(jnp.int32, (table.shape[0], D_HEAD), 0) == residue
            here = lax.broadcasted_iota(jnp.int32, (16, D_HEAD), 0) == local - base
            for dest in range(seq_devices):
                for head in range(HEADS_LOCAL):
                    start = dest * wide + head * D_HEAD
                    picked = table_ref[:, start : start + D_HEAD].astype(jnp.float32)
                    added = jnp.sum(jnp.where(picks, picked, 0.0), axis=0, keepdims=True)
                    now = g_ref[pl.ds(base, 16), start : start + D_HEAD].astype(jnp.float32)
                    outs[head][dest, pl.ds(pl.multiple_of(bases[head] + base, 16), 16), :] = (
                        now + jnp.where(here, added, 0.0)
                    ).astype(jnp.bfloat16)

    near = pl.BlockSpec((rows, width), lambda g, numbers_ref: (numbers_ref[0], 0))
    far = pl.BlockSpec((rows, width), lambda g, numbers_ref: (numbers_ref[1], 0))
    dims = [(seq_devices, base + toks, D_HEAD) for base in bases]
    return pl.pallas_call(
        body,
        grid_spec=pltpu.PrefetchScalarGridSpec(
            num_scalar_prefetch=1,
            grid=(1,),
            in_specs=[near, near, near, far, far, far]
            + [
                pl.BlockSpec((toks, width), lambda g, s: (0, 0)),
                pl.BlockSpec(table.shape, lambda g, s: (0, 0)),
            ],
            out_specs=[pl.BlockSpec(d, lambda g, s: (0, 0, 0)) for d in dims],
        ),
        out_shape=[jax.ShapeDtypeStruct(d, jnp.bfloat16) for d in dims],
        cost_estimate=pl.CostEstimate(
            flops=5_000_000_000, transcendentals=0, bytes_accessed=4 * toks * width
        ),
        name="pack_rest",
    )(numbers, queries, keys, values, queries, keys, values, grad_out, table)


def dot_nt(left, right):
    return lax.dot_general(left, right, (((1,), (1,)), ((), ())), preferred_element_type=jnp.float32)


def dot_nn(left, right):
    return lax.dot_general(left, right, (((1,), (0,)), ((), ())), preferred_element_type=jnp.float32)


def attention(head, tiles, counts, order, sources, arrays, parts, cot, toks, row_devices):
    seq_devices = arrays[0].shape[0]
    rows = toks // row_devices
    block_count = seq_devices * toks // BLOCK
    per_dev = toks // BLOCK
    quarters = BLOCK // rows
    n_arrays = len(arrays)
    n_in = 1 + 3 * len(parts)
    many = 4

    def body(tiles_ref, counts_ref, order_ref, source_ref, *refs):
        array_refs = refs[:n_arrays]
        out_hbm = refs[n_arrays]
        q_v, kv_v, c_v, kt_v, grads_v, out_ref, even_s, odd_s, even_t, odd_t, sem = refs[
            n_arrays + 1 :
        ]
        found_v, terms_v = (even_s, odd_s), (even_t, odd_t)
        lanes = (None, pl.ds(0, D_HEAD), pl.ds(D_HEAD, D_HEAD))
        copies = []
        for p, (which_array, begin_row, devs) in enumerate(parts):
            share = source_ref[p]
            for which in range(3):
                if which == 0:
                    dst = q_v.at[pl.ds(*devs), share // quarters, share % quarters]
                else:
                    dst = kv_v.at[
                        pl.ds(*devs), share // quarters, share % quarters, :, lanes[which]
                    ]
                src = array_refs[which_array].at[:, pl.ds(begin_row + which * rows, rows)]
                copies.append(pltpu.make_async_copy(src, dst, sem.at[3 * p + which]))
        copies.append(
            pltpu.make_async_copy(
                array_refs[cot[0]].at[:, pl.ds(cot[1], toks)], c_v, sem.at[n_in - 1]
            )
        )
        for copy in copies:
            copy.start()

        def clear(b, carry):
            grads_v[b] = jnp.zeros((BLOCK, 2 * D_HEAD), jnp.float32)
            return carry

        for ref in found_v + terms_v:
            ref[...] = jnp.zeros(ref.shape, ref.dtype)

        lax.fori_loop(0, block_count, clear, 0)
        for copy in copies:
            copy.wait()

        def flip(g, carry):
            for n in range(many):
                b = g * many + n
                block = kv_v[b // per_dev, b % per_dev, :, :, :D_HEAD]
                kt_v[b] = block.reshape(BLOCK, D_HEAD).T
            return carry

        lax.fori_loop(0, block_count // many, flip, 0)

        def at_block(b):
            return pl.ds(pl.multiple_of((b % per_dev) * BLOCK, BLOCK), BLOCK)

        def tile_of(i, j):
            return jnp.where(j < counts_ref[i], tiles_ref[i * TILES + j], i)

        def begin(i, count, found_ref):
            q_b = q_v[i // per_dev, i % per_dev].reshape(BLOCK, D_HEAD)
            c_b = c_v[i // per_dev, at_block(i), :]
            ids = [tile_of(i, j) for j in range(count)]
            blocks = [kv_v[t // per_dev, t % per_dev] for t in ids]
            k_all = jnp.concatenate(
                [x[:, :, :D_HEAD].reshape(BLOCK, D_HEAD) for x in blocks], axis=0
            )
            v_all = jnp.concatenate(
                [x[:, :, D_HEAD:].reshape(BLOCK, D_HEAD) for x in blocks], axis=0
            )
            found_ref[: count * BLOCK, :D_HEAD] = dot_nt(k_all, q_b)
            found_ref[: count * BLOCK, D_HEAD:] = dot_nt(v_all, c_b)

        def middle(used, count, found_ref, terms_ref):
            cuts = [slice(j * BLOCK, (j + 1) * BLOCK) for j in range(count)]
            tops = [
                jnp.where(j < used, jnp.max(found_ref[c, :D_HEAD], axis=0, keepdims=True), -jnp.inf)
                for j, c in enumerate(cuts)
            ]
            top = functools.reduce(jnp.maximum, tops) * EXP_SCALE
            total, delta, probs = 0.0, 0.0, []
            for j, c in enumerate(cuts):
                shift = jnp.where(j < used, top, jnp.inf)
                p = jnp.exp2(found_ref[c, :D_HEAD] * EXP_SCALE - shift)
                total = total + p
                delta = delta + p * found_ref[c, D_HEAD:]
                probs.append(p)
            total = jnp.sum(total, axis=0, keepdims=True)
            inverse = jnp.where(used > 0, 1.0 / total, 0.0)
            delta = jnp.sum(delta, axis=0, keepdims=True) * inverse
            for c, p in zip(cuts, probs):
                p = p * inverse
                terms_ref[c, :D_HEAD] = (p * (found_ref[c, D_HEAD:] - delta)).astype(jnp.bfloat16)
                terms_ref[c, D_HEAD:] = p.astype(jnp.bfloat16)

        def end(i, count, terms_ref):
            q_b = q_v[i // per_dev, i % per_dev].reshape(BLOCK, D_HEAD)
            c_b = c_v[i // per_dev, at_block(i), :]
            ids = [tile_of(i, j) for j in range(count)]
            scores = terms_ref[: count * BLOCK, :D_HEAD]
            probs = terms_ref[: count * BLOCK, D_HEAD:]
            key_terms = dot_nn(scores, q_b)
            value_terms = dot_nn(probs, c_b)
            grad_q = dot_nn(jnp.concatenate([kt_v[t] for t in ids], axis=1), scores)
            for j, t in enumerate(ids):
                grads_v[t, :, :D_HEAD] += key_terms[j * BLOCK : (j + 1) * BLOCK]
                grads_v[t, :, D_HEAD:] += value_terms[j * BLOCK : (j + 1) * BLOCK]
            out_ref[i // per_dev, 0, at_block(i), :] = (grad_q.T * SCALE).astype(jnp.bfloat16)

        def step(half, carry):
            for parity in range(2):
                g = 2 * half + parity
                first = order_ref[jnp.minimum(g, block_count - 1)]
                second = order_ref[jnp.clip(g - 1, 0, block_count - 1)]
                third = order_ref[jnp.maximum(g - 2, 0)]
                used = jnp.where(g > 0, counts_ref[second], 0)
                most = counts_ref[third]

                def choose(low, high, first, second, third, used, most, parity):
                    if low == high:
                        end(third, low, terms_v[parity])
                        middle(used, low, found_v[1 - parity], terms_v[1 - parity])
                        begin(first, low, found_v[parity])
                        return
                    split = (low + high) // 2

                    @pl.when(most <= split)
                    def _():
                        choose(low, split, first, second, third, used, most, parity)

                    @pl.when(most > split)
                    def _():
                        choose(split + 1, high, first, second, third, used, most, parity)

                choose(1, TILES, first, second, third, used, most, parity)

            return carry

        lax.fori_loop(0, block_count // 2 + 1, step, 0)

        stored = [pltpu.make_async_copy(out_ref.at[:, 0], out_hbm.at[:, 0], sem.at[n_in])]
        stored[0].start()
        quarter = seq_devices // many
        for part in range(many):

            def finish(dev, carry):
                for n in range(per_dev):
                    grads = grads_v[dev * per_dev + n]
                    at = pl.ds(n * BLOCK, BLOCK)
                    out_ref[dev, 1, at, :] = (grads[:, :D_HEAD] * SCALE).astype(jnp.bfloat16)
                    out_ref[dev, 2, at, :] = grads[:, D_HEAD:].astype(jnp.bfloat16)
                return carry

            lax.fori_loop(part * quarter, (part + 1) * quarter, finish, 0)
            at = (pl.ds(part * quarter, quarter), pl.ds(1, 2))
            stored.append(
                pltpu.make_async_copy(out_ref.at[at], out_hbm.at[at], sem.at[n_in + 1 + part])
            )
            stored[-1].start()
        for copy in stored:
            copy.wait()

    token_dims = (seq_devices, per_dev, quarters, rows)
    out_dims = (seq_devices, 3, toks, D_HEAD)
    return pl.pallas_call(
        body,
        grid_spec=pltpu.PrefetchScalarGridSpec(
            num_scalar_prefetch=4,
            grid=(1,),
            in_specs=[pl.BlockSpec(memory_space=pl.ANY)] * n_arrays,
            out_specs=pl.BlockSpec(memory_space=pltpu.HBM),
            scratch_shapes=[
                pltpu.VMEM(token_dims + (D_HEAD,), jnp.bfloat16),
                pltpu.VMEM(token_dims + (2 * D_HEAD,), jnp.bfloat16),
                pltpu.VMEM((seq_devices, toks, D_HEAD), jnp.bfloat16),
                pltpu.VMEM((block_count, D_HEAD, BLOCK), jnp.bfloat16),
                pltpu.VMEM((block_count, BLOCK, 2 * D_HEAD), jnp.float32),
                pltpu.VMEM(out_dims, jnp.bfloat16),
                pltpu.VMEM((TILES * BLOCK, 2 * D_HEAD), jnp.float32),
                pltpu.VMEM((TILES * BLOCK, 2 * D_HEAD), jnp.float32),
                pltpu.VMEM((TILES * BLOCK, 2 * D_HEAD), jnp.bfloat16),
                pltpu.VMEM((TILES * BLOCK, 2 * D_HEAD), jnp.bfloat16),
                pltpu.SemaphoreType.DMA((n_in + 1 + many,)),
            ],
        ),
        out_shape=pltpu.HBM(out_dims, jnp.bfloat16),
        compiler_params=pltpu.CompilerParams(vmem_limit_bytes=32 << 20),
        cost_estimate=pl.CostEstimate(
            flops=(40_000_000_000, 1_000_000)[head], transcendentals=0, bytes_accessed=1 << 20
        ),
    )(tiles, counts, order, sources, *arrays)


def unpack(head, arrived, outs, seq_devices):
    toks = arrived.shape[2]
    wide = HEADS_LOCAL * D_HEAD
    dims = (toks, seq_devices * wide)

    def body(src, *refs):
        dsts = refs[-4:-1]
        sem = refs[-1]
        copies = []
        for which in range(3):
            for dev in range(seq_devices):
                copies.append(
                    pltpu.make_async_copy(
                        src.at[dev, which],
                        dsts[which].at[:, pl.ds(dev * wide + head * D_HEAD, D_HEAD)],
                        sem.at[which * seq_devices + dev],
                    )
                )
        for copy in copies:
            copy.start()
        for copy in copies:
            copy.wait()

    return pl.pallas_call(
        body,
        in_specs=[pl.BlockSpec(memory_space=pl.ANY if outs else pltpu.VMEM)]
        + [pl.BlockSpec(memory_space=pl.ANY)] * len(outs),
        out_specs=[pl.BlockSpec(memory_space=pl.ANY)] * 3,
        out_shape=[jax.ShapeDtypeStruct(dims, jnp.bfloat16)] * 3,
        scratch_shapes=[pltpu.SemaphoreType.DMA((3 * seq_devices,))],
        input_output_aliases={1 + n: n for n in range(len(outs))},
        compiler_params=pltpu.CompilerParams(vmem_limit_bytes=8 << 20),
    )(arrived, *outs)


def per_device(queries, keys, values, grad_out, table, positions, residues, tiles, counts):
    toks = queries.shape[0]
    row_devices = lax.axis_size("rows")
    seq_devices = lax.axis_size("seq")
    row = lax.axis_index("rows").astype(jnp.int32)
    first = lax.axis_index("seq").astype(jnp.int32) * toks
    chips = row_devices // 2
    spread = lambda x: lax.all_to_all(x, "seq", split_axis=0, concat_axis=0, tiled=True)

    def shift(x, hops):
        pairs = [
            (z * 2 + c, ((z + hops) % chips) * 2 + c) for z in range(chips) for c in range(2)
        ]
        return lax.ppermute(x, "rows", pairs)

    def swap(x):
        return lax.ppermute(x, "rows", [(n, n ^ 1) for n in range(row_devices)])

    half = row_devices // 2
    rows = toks // row_devices
    numbers = jnp.stack([row, (row + half) % row_devices, positions[0] - first, residues[0]])
    own = pack_first(row[None], queries, keys, values, row_devices, seq_devices)
    cot, late = pack_rest(
        numbers, queries, keys, values, grad_out[0], table, row_devices, seq_devices
    )
    own = spread(own)
    flip = row ^ 1
    sources = [
        [row, flip, row - 2, row + 2, row + half, flip - 2, flip + 2, flip + half],
        [row, row + half, flip, flip + half, row - 2, row + 2, flip - 2, flip + 2],
    ]
    sources = [jnp.stack(x) % row_devices for x in sources]
    everyone = (0, seq_devices)
    parts = [
        [(n, 0, everyone) for n in range(8)],
        [(0, 0, everyone), (0, 3 * rows, everyone), (1, 0, everyone), (1, 3 * rows, everyone)]
        + [(n, 0, everyone) for n in range(2, 6)],
    ]

    blocks = jnp.arange(counts.shape[0], dtype=jnp.int32)
    ahead_of = (counts[None, :] > counts[:, None]) | (
        (counts[None, :] == counts[:, None]) & (blocks[None, :] < blocks[:, None])
    )
    place = jnp.sum(ahead_of.astype(jnp.int32), axis=1)
    order = jnp.sum(jnp.where(place[None, :] == blocks[:, None], blocks[None, :], 0), axis=1)

    def gather(near):
        back, ahead = shift(near, 1), shift(near, -1)
        return [back, ahead, swap(back), swap(ahead)]

    def work(head, arrays, cot_at):
        return attention(
            head,
            tiles.reshape(-1),
            counts,
            order,
            sources[head],
            arrays,
            parts[head],
            cot_at,
            toks,
            row_devices,
        )

    own, cot, late = lax.optimization_barrier((own, cot, late))
    back, ahead = shift(own, 1), shift(own, -1)
    sides = [back, ahead, shift(back, 1)]
    arrays = [own, swap(own)] + sides
    arrays = arrays + [swap(x) for x in sides]
    cot = spread(cot)
    late = spread(late)
    grads = work(0, arrays + [cot], (8, 0))
    grads, late = lax.optimization_barrier((grads, late))
    first_out = spread(grads)
    arrays = [late, swap(late[:, : 6 * rows])] + gather(late[:, : 3 * rows])
    grads = work(1, arrays, (0, 6 * rows))
    outs = unpack(0, first_out, [], seq_devices)
    outs = unpack(1, spread(grads), outs, seq_devices)
    return tuple(x[None] for x in outs)


def solution(mesh):
    placed = (
        P("seq", None),
        P("seq", None),
        P("seq", None),
        P("rows", "seq", None),
        P(),
        P("rows"),
        P("rows"),
        P(),
        P(),
    )

    return jax.shard_map(
        per_device,
        mesh=mesh,
        in_specs=placed,
        out_specs=(P("rows", "seq", None), P("rows", "seq", None), P("rows", "seq", None)),
        check_vma=False,
    )
```

```python
import functools
import math

import jax
import jax.numpy as jnp
from jax import lax
from jax.experimental import pallas as pl
from jax.experimental.pallas import tpu as pltpu
from jax.sharding import PartitionSpec as P

D_HEAD = 128
BLOCK = 128
TILES = 8
HEADS_LOCAL = 2
SCALE = D_HEAD ** (-0.5)
EXP_SCALE = SCALE * math.log2(math.e)


def pack_first(share, queries, keys, values, row_devices, seq_devices):
    toks, width = queries.shape
    rows = toks // row_devices
    wide = HEADS_LOCAL * D_HEAD

    def body(share_ref, *refs):
        out_ref = refs[-1]
        for n, ref in enumerate(refs[:-1]):
            for dest in range(seq_devices):
                start = dest * wide
                out_ref[dest, n * rows : (n + 1) * rows] = ref[:, start : start + D_HEAD]

    near = pl.BlockSpec((rows, width), lambda g, share_ref: (share_ref[0], 0))
    out_dims = (seq_devices, 3 * rows, D_HEAD)
    return pl.pallas_call(
        body,
        grid_spec=pltpu.PrefetchScalarGridSpec(
            num_scalar_prefetch=1,
            grid=(1,),
            in_specs=[near, near, near],
            out_specs=pl.BlockSpec(out_dims, lambda g, share_ref: (0, 0, 0)),
        ),
        out_shape=jax.ShapeDtypeStruct(out_dims, jnp.bfloat16),
        name="pack_first",
    )(share, queries, keys, values)


def pack_rest(numbers, queries, keys, values, grad_out, table, row_devices, seq_devices):
    toks, width = grad_out.shape
    rows = toks // row_devices
    wide = HEADS_LOCAL * D_HEAD
    bases = (0, 6 * rows)

    def body(numbers_ref, *refs):
        share_refs = refs[:6]
        g_ref, table_ref = refs[6:8]
        outs = refs[8:]
        local = numbers_ref[2]
        residue = numbers_ref[3]
        for dest in range(seq_devices):
            for n, ref in enumerate(share_refs):
                start = dest * wide + D_HEAD
                outs[1][dest, n * rows : (n + 1) * rows] = ref[:, start : start + D_HEAD]
            for head in range(HEADS_LOCAL):
                start = dest * wide + head * D_HEAD
                outs[head][dest, bases[head] : bases[head] + toks] = g_ref[
                    :, start : start + D_HEAD
                ]

        @pl.when(jnp.logical_and(local >= 0, local < toks))
        def _():
            base = pl.multiple_of((local // 16) * 16, 16)
            picks = lax.broadcasted_iota(jnp.int32, (table.shape[0], D_HEAD), 0) == residue
            here = lax.broadcasted_iota(jnp.int32, (16, D_HEAD), 0) == local - base
            for dest in range(seq_devices):
                for head in range(HEADS_LOCAL):
                    start = dest * wide + head * D_HEAD
                    picked = table_ref[:, start : start + D_HEAD].astype(jnp.float32)
                    added = jnp.sum(jnp.where(picks, picked, 0.0), axis=0, keepdims=True)
                    now = g_ref[pl.ds(base, 16), start : start + D_HEAD].astype(jnp.float32)
                    outs[head][dest, pl.ds(pl.multiple_of(bases[head] + base, 16), 16), :] = (
                        now + jnp.where(here, added, 0.0)
                    ).astype(jnp.bfloat16)

    near = pl.BlockSpec((rows, width), lambda g, numbers_ref: (numbers_ref[0], 0))
    far = pl.BlockSpec((rows, width), lambda g, numbers_ref: (numbers_ref[1], 0))
    dims = [(seq_devices, base + toks, D_HEAD) for base in bases]
    return pl.pallas_call(
        body,
        grid_spec=pltpu.PrefetchScalarGridSpec(
            num_scalar_prefetch=1,
            grid=(1,),
            in_specs=[near, near, near, far, far, far]
            + [
                pl.BlockSpec((toks, width), lambda g, s: (0, 0)),
                pl.BlockSpec(table.shape, lambda g, s: (0, 0)),
            ],
            out_specs=[pl.BlockSpec(d, lambda g, s: (0, 0, 0)) for d in dims],
        ),
        out_shape=[jax.ShapeDtypeStruct(d, jnp.bfloat16) for d in dims],
        cost_estimate=pl.CostEstimate(
            flops=5_000_000_000, transcendentals=0, bytes_accessed=4 * toks * width
        ),
        name="pack_rest",
    )(numbers, queries, keys, values, queries, keys, values, grad_out, table)


def dot_nt(left, right):
    return lax.dot_general(left, right, (((1,), (1,)), ((), ())), preferred_element_type=jnp.float32)


def dot_nn(left, right):
    return lax.dot_general(left, right, (((1,), (0,)), ((), ())), preferred_element_type=jnp.float32)


def attention(head, tiles, counts, order, sources, arrays, parts, cot, toks, row_devices):
    seq_devices = arrays[0].shape[0]
    rows = toks // row_devices
    block_count = seq_devices * toks // BLOCK
    per_dev = toks // BLOCK
    quarters = BLOCK // rows
    n_arrays = len(arrays)
    n_in = 1 + 3 * len(parts)
    many = 4

    def body(tiles_ref, counts_ref, order_ref, source_ref, *refs):
        array_refs = refs[:n_arrays]
        out_hbm = refs[n_arrays]
        q_v, kv_v, c_v, kt_v, grads_v, out_ref, even_s, odd_s, even_t, odd_t, sem = refs[
            n_arrays + 1 :
        ]
        found_v, terms_v = (even_s, odd_s), (even_t, odd_t)
        lanes = (None, pl.ds(0, D_HEAD), pl.ds(D_HEAD, D_HEAD))
        copies = []
        for p, (which_array, begin_row, devs) in enumerate(parts):
            share = source_ref[p]
            for which in range(3):
                if which == 0:
                    dst = q_v.at[pl.ds(*devs), share // quarters, share % quarters]
                else:
                    dst = kv_v.at[
                        pl.ds(*devs), share // quarters, share % quarters, :, lanes[which]
                    ]
                src = array_refs[which_array].at[:, pl.ds(begin_row + which * rows, rows)]
                copies.append(pltpu.make_async_copy(src, dst, sem.at[3 * p + which]))
        copies.append(
            pltpu.make_async_copy(
                array_refs[cot[0]].at[:, pl.ds(cot[1], toks)], c_v, sem.at[n_in - 1]
            )
        )
        for copy in copies:
            copy.start()

        def clear(b, carry):
            grads_v[b] = jnp.zeros((BLOCK, 2 * D_HEAD), jnp.float32)
            return carry

        for ref in found_v + terms_v:
            ref[...] = jnp.zeros(ref.shape, ref.dtype)

        lax.fori_loop(0, block_count, clear, 0)
        for copy in copies:
            copy.wait()

        def flip(g, carry):
            for n in range(many):
                b = g * many + n
                block = kv_v[b // per_dev, b % per_dev, :, :, :D_HEAD]
                kt_v[b] = block.reshape(BLOCK, D_HEAD).T
            return carry

        lax.fori_loop(0, block_count // many, flip, 0)

        def at_block(b):
            return pl.ds(pl.multiple_of((b % per_dev) * BLOCK, BLOCK), BLOCK)

        def tile_of(i, j):
            return jnp.where(j < counts_ref[i], tiles_ref[i * TILES + j], i)

        def begin(i, count, found_ref):
            q_b = q_v[i // per_dev, i % per_dev].reshape(BLOCK, D_HEAD)
            c_b = c_v[i // per_dev, at_block(i), :]
            ids = [tile_of(i, j) for j in range(count)]
            blocks = [kv_v[t // per_dev, t % per_dev] for t in ids]
            k_all = jnp.concatenate(
                [x[:, :, :D_HEAD].reshape(BLOCK, D_HEAD) for x in blocks], axis=0
            )
            v_all = jnp.concatenate(
                [x[:, :, D_HEAD:].reshape(BLOCK, D_HEAD) for x in blocks], axis=0
            )
            found_ref[: count * BLOCK, :D_HEAD] = dot_nt(k_all, q_b)
            found_ref[: count * BLOCK, D_HEAD:] = dot_nt(v_all, c_b)

        def middle(used, count, found_ref, terms_ref):
            cuts = [slice(j * BLOCK, (j + 1) * BLOCK) for j in range(count)]
            tops = [
                jnp.where(j < used, jnp.max(found_ref[c, :D_HEAD], axis=0, keepdims=True), -jnp.inf)
                for j, c in enumerate(cuts)
            ]
            top = functools.reduce(jnp.maximum, tops) * EXP_SCALE
            total, delta, probs = 0.0, 0.0, []
            for j, c in enumerate(cuts):
                shift = jnp.where(j < used, top, jnp.inf)
                p = jnp.exp2(found_ref[c, :D_HEAD] * EXP_SCALE - shift)
                total = total + p
                delta = delta + p * found_ref[c, D_HEAD:]
                probs.append(p)
            total = jnp.sum(total, axis=0, keepdims=True)
            inverse = jnp.where(used > 0, 1.0 / total, 0.0)
            delta = jnp.sum(delta, axis=0, keepdims=True) * inverse
            for c, p in zip(cuts, probs):
                p = p * inverse
                terms_ref[c, :D_HEAD] = (p * (found_ref[c, D_HEAD:] - delta)).astype(jnp.bfloat16)
                terms_ref[c, D_HEAD:] = p.astype(jnp.bfloat16)

        def end(i, count, terms_ref):
            q_b = q_v[i // per_dev, i % per_dev].reshape(BLOCK, D_HEAD)
            c_b = c_v[i // per_dev, at_block(i), :]
            ids = [tile_of(i, j) for j in range(count)]
            scores = terms_ref[: count * BLOCK, :D_HEAD]
            probs = terms_ref[: count * BLOCK, D_HEAD:]
            key_terms = dot_nn(scores, q_b)
            value_terms = dot_nn(probs, c_b)
            grad_q = dot_nn(jnp.concatenate([kt_v[t] for t in ids], axis=1), scores)
            for j, t in enumerate(ids):
                grads_v[t, :, :D_HEAD] += key_terms[j * BLOCK : (j + 1) * BLOCK]
                grads_v[t, :, D_HEAD:] += value_terms[j * BLOCK : (j + 1) * BLOCK]
            out_ref[i // per_dev, 0, at_block(i), :] = (grad_q.T * SCALE).astype(jnp.bfloat16)

        def step(half, carry):
            for parity in range(2):
                g = 2 * half + parity
                first = order_ref[jnp.minimum(g, block_count - 1)]
                second = order_ref[jnp.clip(g - 1, 0, block_count - 1)]
                third = order_ref[jnp.maximum(g - 2, 0)]
                used = jnp.where(g > 0, counts_ref[second], 0)
                most = counts_ref[third]

                def choose(low, high, first, second, third, used, most, parity):
                    if low == high:
                        end(third, low, terms_v[parity])
                        middle(used, low, found_v[1 - parity], terms_v[1 - parity])
                        begin(first, low, found_v[parity])
                        return
                    split = (low + high) // 2

                    @pl.when(most <= split)
                    def _():
                        choose(low, split, first, second, third, used, most, parity)

                    @pl.when(most > split)
                    def _():
                        choose(split + 1, high, first, second, third, used, most, parity)

                choose(1, TILES, first, second, third, used, most, parity)

            return carry

        lax.fori_loop(0, block_count // 2 + 1, step, 0)

        stored = [pltpu.make_async_copy(out_ref.at[:, 0], out_hbm.at[:, 0], sem.at[n_in])]
        stored[0].start()
        quarter = seq_devices // many
        for part in range(many):

            def finish(dev, carry):
                for n in range(per_dev):
                    grads = grads_v[dev * per_dev + n]
                    at = pl.ds(n * BLOCK, BLOCK)
                    out_ref[dev, 1, at, :] = (grads[:, :D_HEAD] * SCALE).astype(jnp.bfloat16)
                    out_ref[dev, 2, at, :] = grads[:, D_HEAD:].astype(jnp.bfloat16)
                return carry

            lax.fori_loop(part * quarter, (part + 1) * quarter, finish, 0)
            at = (pl.ds(part * quarter, quarter), pl.ds(1, 2))
            stored.append(
                pltpu.make_async_copy(out_ref.at[at], out_hbm.at[at], sem.at[n_in + 1 + part])
            )
            stored[-1].start()
        for copy in stored:
            copy.wait()

    token_dims = (seq_devices, per_dev, quarters, rows)
    out_dims = (seq_devices, 3, toks, D_HEAD)
    return pl.pallas_call(
        body,
        grid_spec=pltpu.PrefetchScalarGridSpec(
            num_scalar_prefetch=4,
            grid=(1,),
            in_specs=[pl.BlockSpec(memory_space=pl.ANY)] * n_arrays,
            out_specs=pl.BlockSpec(memory_space=pltpu.HBM),
            scratch_shapes=[
                pltpu.VMEM(token_dims + (D_HEAD,), jnp.bfloat16),
                pltpu.VMEM(token_dims + (2 * D_HEAD,), jnp.bfloat16),
                pltpu.VMEM((seq_devices, toks, D_HEAD), jnp.bfloat16),
                pltpu.VMEM((block_count, D_HEAD, BLOCK), jnp.bfloat16),
                pltpu.VMEM((block_count, BLOCK, 2 * D_HEAD), jnp.float32),
                pltpu.VMEM(out_dims, jnp.bfloat16),
                pltpu.VMEM((TILES * BLOCK, 2 * D_HEAD), jnp.float32),
                pltpu.VMEM((TILES * BLOCK, 2 * D_HEAD), jnp.float32),
                pltpu.VMEM((TILES * BLOCK, 2 * D_HEAD), jnp.bfloat16),
                pltpu.VMEM((TILES * BLOCK, 2 * D_HEAD), jnp.bfloat16),
                pltpu.SemaphoreType.DMA((n_in + 1 + many,)),
            ],
        ),
        out_shape=pltpu.HBM(out_dims, jnp.bfloat16),
        compiler_params=pltpu.CompilerParams(vmem_limit_bytes=32 << 20),
        cost_estimate=pl.CostEstimate(
            flops=(40_000_000_000, 1_000_000)[head], transcendentals=0, bytes_accessed=1 << 20
        ),
    )(tiles, counts, order, sources, *arrays)


def unpack(head, arrived, outs, seq_devices):
    toks = arrived.shape[2]
    wide = HEADS_LOCAL * D_HEAD
    dims = (toks, seq_devices * wide)

    def body(src, *refs):
        dsts = refs[-4:-1]
        sem = refs[-1]
        copies = []
        for which in range(3):
            for dev in range(seq_devices):
                copies.append(
                    pltpu.make_async_copy(
                        src.at[dev, which],
                        dsts[which].at[:, pl.ds(dev * wide + head * D_HEAD, D_HEAD)],
                        sem.at[which * seq_devices + dev],
                    )
                )
        for copy in copies:
            copy.start()
        for copy in copies:
            copy.wait()

    return pl.pallas_call(
        body,
        in_specs=[pl.BlockSpec(memory_space=pl.ANY if outs else pltpu.VMEM)]
        + [pl.BlockSpec(memory_space=pl.ANY)] * len(outs),
        out_specs=[pl.BlockSpec(memory_space=pl.ANY)] * 3,
        out_shape=[jax.ShapeDtypeStruct(dims, jnp.bfloat16)] * 3,
        scratch_shapes=[pltpu.SemaphoreType.DMA((3 * seq_devices,))],
        input_output_aliases={1 + n: n for n in range(len(outs))},
        compiler_params=pltpu.CompilerParams(vmem_limit_bytes=8 << 20),
    )(arrived, *outs)


def per_device(queries, keys, values, grad_out, table, positions, residues, tiles, counts):
    toks = queries.shape[0]
    row_devices = lax.axis_size("rows")
    seq_devices = lax.axis_size("seq")
    row = lax.axis_index("rows").astype(jnp.int32)
    first = lax.axis_index("seq").astype(jnp.int32) * toks
    chips = row_devices // 2
    spread = lambda x: lax.all_to_all(x, "seq", split_axis=0, concat_axis=0, tiled=True)

    def shift(x, hops):
        pairs = [
            (z * 2 + c, ((z + hops) % chips) * 2 + c) for z in range(chips) for c in range(2)
        ]
        return lax.ppermute(x, "rows", pairs)

    def swap(x):
        return lax.ppermute(x, "rows", [(n, n ^ 1) for n in range(row_devices)])

    half = row_devices // 2
    rows = toks // row_devices
    numbers = jnp.stack([row, (row + half) % row_devices, positions[0] - first, residues[0]])
    own = pack_first(row[None], queries, keys, values, row_devices, seq_devices)
    cot, late = pack_rest(
        numbers, queries, keys, values, grad_out[0], table, row_devices, seq_devices
    )
    own = spread(own)
    flip = row ^ 1
    sources = [
        [row, flip, row - 2, row + 2, flip - 2, flip + 2] + [row + half] * 2 + [flip + half] * 2,
        [row, row + half, flip, flip + half, row - 2, row + 2, flip - 2, flip + 2],
    ]
    sources = [jnp.stack(x) % row_devices for x in sources]
    everyone = (0, seq_devices)
    lows, highs = (0, seq_devices // 2), (seq_devices // 2, seq_devices // 2)
    parts = [
        [(n, 0, everyone) for n in range(6)]
        + [(6, 0, lows), (7, 0, highs), (8, 0, lows), (9, 0, highs)],
        [(0, 0, everyone), (0, 3 * rows, everyone), (1, 0, everyone), (1, 3 * rows, everyone)]
        + [(n, 0, everyone) for n in range(2, 6)],
    ]

    blocks = jnp.arange(counts.shape[0], dtype=jnp.int32)
    ahead_of = (counts[None, :] > counts[:, None]) | (
        (counts[None, :] == counts[:, None]) & (blocks[None, :] < blocks[:, None])
    )
    place = jnp.sum(ahead_of.astype(jnp.int32), axis=1)
    order = jnp.sum(jnp.where(place[None, :] == blocks[:, None], blocks[None, :], 0), axis=1)

    def gather(near):
        back, ahead = shift(near, 1), shift(near, -1)
        return [back, ahead, swap(back), swap(ahead)]

    def work(head, arrays, cot_at):
        return attention(
            head,
            tiles.reshape(-1),
            counts,
            order,
            sources[head],
            arrays,
            parts[head],
            cot_at,
            toks,
            row_devices,
        )

    own, cot, late = lax.optimization_barrier((own, cot, late))
    back, ahead = shift(own, 1), shift(own, -1)
    arrays = [own, swap(own), back, ahead]
    arrays = arrays + [swap(back), swap(ahead)]
    far = [shift(back[: seq_devices // 2], 1), shift(ahead[seq_devices // 2 :], -1)]
    arrays = arrays + far + [swap(x) for x in far]
    cot = spread(cot)
    late = spread(late)
    grads = work(0, arrays + [cot], (10, 0))
    grads, late = lax.optimization_barrier((grads, late))
    first_out = spread(grads)
    arrays = [late, swap(late[:, : 6 * rows])] + gather(late[:, : 3 * rows])
    grads = work(1, arrays, (0, 6 * rows))
    outs = unpack(0, first_out, [], seq_devices)
    outs = unpack(1, spread(grads), outs, seq_devices)
    return tuple(x[None] for x in outs)


def solution(mesh):
    placed = (
        P("seq", None),
        P("seq", None),
        P("seq", None),
        P("rows", "seq", None),
        P(),
        P("rows"),
        P("rows"),
        P(),
        P(),
    )

    return jax.shard_map(
        per_device,
        mesh=mesh,
        in_specs=placed,
        out_specs=(P("rows", "seq", None), P("rows", "seq", None), P("rows", "seq", None)),
        check_vma=False,
    )
```
